128 devices in a mesh: ctx: 16 (over x_lo, z, core), head: 8 (over x_hi, y).
Axes of the slice: x: 4 (x_hi: 2, x_lo: 2; x = x_hi * 2 + x_lo), y: 4, z: 4, core: 2. Of those that a mesh axis runs over, the one named last changes fastest.
Arguments:
- queries: bfloat16 [4096, 4096], P(('ctx', 'head')), may hold values from -10 to 10
- keys: bfloat16 [4096, 4096], P(('ctx', 'head')), may hold values from -10 to 10
- values: bfloat16 [4096, 4096], P(('ctx', 'head')), may hold values from -6 to 6
- grad_out: bfloat16 [4096, 4096], P(('ctx', 'head')), may hold values from -6 to 6
- block_doc: int32 [32], replicated, may hold values from 0 to 7, as said below
Outputs:
- attn_out: bfloat16 [4096, 4096], P(('ctx', 'head'))
- d_q: bfloat16 [4096, 4096], P(('ctx', 'head'))
- d_k: bfloat16 [4096, 4096], P(('ctx', 'head'))
- d_v: bfloat16 [4096, 4096], P(('ctx', 'head'))
The draws below stay inside these ranges and needn't reach their ends.
Inputs may be any that keep to these rules, and one draw needn't show every extreme that they name: `block_doc`: document numbers never fall; every document covers at least one block; the last document covers exactly 16 blocks and every other one fewer.
All inputs are finite; a program needn't handle non-finite values.
Results may differ from the reference program's by a relative error of at most 0.03.
Values may be sent and summed in bfloat16 or wider, within the bound.
No kernel may reach another device: no remote copies, remote signals or barrier semaphores. Data moves between devices by JAX's collectives and lax.ppermute only.
A program may use at most 128 MiB of HBM per device.

```python
from functools import partial
import jax
import jax.numpy as jnp
from jax import lax

HEADS = 32
HD = 128
TOK_DEV = 256
BLK = 128
TOKENS = 4096
BLOCKS = 32
DOCS = 8
LONGEST = 16
N_CTX = 16


def draw_queries(key, part):
    base = jax.random.truncated_normal(jax.random.fold_in(key, 11), -6.0, 6.0, (TOKENS, HEADS * HD))
    return base.astype(jnp.bfloat16)


def draw_keys(key, part):
    base = jax.random.truncated_normal(jax.random.fold_in(key, 12), -6.0, 6.0, (TOKENS, HEADS * HD))
    return base.astype(jnp.bfloat16)


def draw_block_doc(key, part):
    earlier = BLOCKS - LONGEST
    order = jax.random.permutation(jax.random.fold_in(key, 41), earlier - 1) + 1
    cuts = order[:DOCS - 2]
    blocks = lax.iota(jnp.int32, BLOCKS)
    numbers = jnp.sum((cuts[None, :] <= blocks[:, None]).astype(jnp.int32), axis=1)
    return jnp.where(blocks >= earlier, DOCS - 1, numbers).astype(jnp.int32)


def level_of(key, extent, cuts, least, top_value):
    loudness, own = 1.0, jax.random.fold_in(key, 6)
    for dim, parts in cuts:
        steps = jnp.exp(jax.random.uniform(jax.random.fold_in(own, dim), (parts,), jnp.float32, least / len(cuts), top_value / len(cuts)))
        loudness = loudness * jnp.repeat(steps, extent[dim] // parts).reshape([-1 if axis == dim else 1 for axis in range(len(extent))])
    return loudness


def scatter_about(rng, extent, deviation, limit, pieces=(), kind=jnp.bfloat16):
    entries = deviation * jax.random.normal(rng, extent, jnp.float32)
    if pieces:
        entries = entries * level_of(rng, extent, pieces, -0.22, 0.18)
    return jnp.clip(entries, -limit, limit).astype(kind)


def setup_inputs(seed: int = 0) -> dict:
    key_of = jax.random.split(jax.random.key(seed), 6)
    queries = draw_queries(jax.random.fold_in(key_of[5], 71), 0)
    keys = draw_keys(jax.random.fold_in(key_of[5], 71), 0)
    values = scatter_about(key_of[2], (TOKENS, HEADS * HD), 1.0, 6.0, ((0, 128),))
    grad_out = scatter_about(key_of[3], (TOKENS, HEADS * HD), 1.0, 6.0, ((0, 128),))
    block_doc = draw_block_doc(jax.random.fold_in(key_of[5], 71), 0)
    return {"queries": queries, "keys": keys, "values": values, "grad_out": grad_out, "block_doc": block_doc}


def one_head(visible, operands):
    query_head, key_head, value_head, grad_head = operands
    score_scale = HD ** -0.5
    scores = jnp.dot(query_head, key_head.T, preferred_element_type=jnp.float32) * score_scale
    row_max = jnp.max(jnp.where(visible, scores, -jnp.inf), axis=1, keepdims=True)
    shifted = jnp.where(visible, jnp.exp(scores - row_max), 0.0)
    total = jnp.sum(shifted, axis=1, keepdims=True)
    log_total = row_max + jnp.log(total)
    out_weights = shifted.astype(jnp.bfloat16)
    attn_head = (jnp.dot(out_weights, value_head, preferred_element_type=jnp.float32) / total).astype(jnp.bfloat16)
    delta = jnp.sum(grad_head.astype(jnp.float32) * attn_head.astype(jnp.float32), axis=1, keepdims=True)
    probs = jnp.where(visible, jnp.exp(scores - log_total), 0.0)
    back_weights = probs.astype(jnp.bfloat16)
    grad_value = jnp.dot(back_weights.T, grad_head, preferred_element_type=jnp.float32).astype(jnp.bfloat16)
    grad_weights = jnp.dot(grad_head, value_head.T, preferred_element_type=jnp.float32)
    grad_scores = (probs * (grad_weights - delta)).astype(jnp.bfloat16)
    grad_query = (jnp.dot(grad_scores, key_head, preferred_element_type=jnp.float32) * score_scale).astype(jnp.bfloat16)
    grad_key = (jnp.dot(grad_scores.T, query_head, preferred_element_type=jnp.float32) * score_scale).astype(jnp.bfloat16)
    return attn_head, grad_query, grad_key, grad_value


def split_heads(array):
    return array.reshape(TOKENS, HEADS, HD).transpose(1, 0, 2)


def join_heads(array):
    return array.transpose(1, 0, 2).reshape(TOKENS, HEADS * HD)


def reference(queries, keys, values, grad_out, block_doc):
    rows = lax.iota(jnp.int32, TOKENS)
    owner = rows // TOK_DEV
    local = rows % TOK_DEV
    half = TOK_DEV // 2
    position = jnp.where(local < half, owner * half + local, (2 * N_CTX - 1 - owner) * half + local - half).astype(jnp.int32)
    document = block_doc[position // BLK]
    visible = (document[:, None] == document[None, :]) & (position[None, :] <= position[:, None])
    results = lax.map(partial(one_head, visible), (split_heads(queries), split_heads(keys), split_heads(values), split_heads(grad_out)))
    return (join_heads(results[0]), join_heads(results[1]), join_heads(results[2]), join_heads(results[3]))
```

```python
import functools

import jax
import jax.numpy as jnp
from jax import lax
from jax.experimental import pallas as pl
from jax.experimental.pallas import tpu as pltpu
from jax.sharding import Mesh, PartitionSpec as P

HD = 128
BLK = 128
SCALE = HD ** (-0.5)
LOG2E = 1.4426950408889634
NEG = -1e30

N_CC = 8
N_Y = 4
GRP = N_CC * N_Y
ROWS = 32
QB = 256
VM = pltpu.VMEM


def pack_kernel(k_ref, v_ref, q_ref, g_ref, o_ref):
    for a, ref in enumerate((k_ref, v_ref, q_ref, g_ref)):
        for h in range(GRP):
            o_ref[h, a] = ref[:, h * HD : (h + 1) * HD]


def unpack_kernel(x_ref, *o_refs):
    for a, ref in enumerate(o_refs):
        for h in range(GRP):
            ref[:, h * HD : (h + 1) * HD] = x_ref[h, a]


def combine_kernel(outdq_ref, own_ref, recv_ref, o_ref):
    o_ref[:, 0:2] = outdq_ref[...]
    o_ref[:, 2:4] = (own_ref[...] + recv_ref[...].astype(jnp.float32)).astype(jnp.bfloat16)


def dot_nt(a, b):
    return lax.dot_general(a, b, (((1,), (1,)), ((), ())), preferred_element_type=jnp.float32)


def dot_nn(a, b):
    return lax.dot_general(a, b, (((1,), (0,)), ((), ())), preferred_element_type=jnp.float32)


def attention_kernel(
    ids_ref, doc_ref, x_ref, oth_ref,
    outdq_ref, own_ref, sent_ref,
    k_own, v_own, k_oth, v_oth, q_all, g_all, acc,
):
    half, core = ids_ref[0], ids_ref[1]
    lead = jnp.where(half == core, 0, 1)

    def slot(t):
        return jnp.where(half == 1, N_CC - 1 - t, t) * N_Y

    for t in range(N_CC):
        rows = slice(t * BLK, (t + 1) * BLK)
        at = pl.ds(slot(t), N_Y)
        k_own[rows] = x_ref[at, 0].reshape(BLK, HD)
        v_own[rows] = x_ref[at, 1].reshape(BLK, HD)
        q_all[rows] = x_ref[at, 2].reshape(BLK, HD)
        g_all[rows] = x_ref[at, 3].reshape(BLK, HD)
        k_oth[rows] = oth_ref[at, 0].reshape(BLK, HD)
        v_oth[rows] = oth_ref[at, 1].reshape(BLK, HD)

    doc_own = [doc_ref[half * 16 + 2 * t + lead] for t in range(N_CC)]
    doc_oth = [doc_ref[half * 16 + 2 * t + 1 - lead] for t in range(N_CC)]

    row = lax.broadcasted_iota(jnp.int32, (BLK, BLK), 0)
    col = lax.broadcasted_iota(jnp.int32, (BLK, BLK), 1)
    below = col <= row

    def masked(s, u, own):
        tall = []
        for i in range(2):
            t = 2 * u + i
            wide = []
            for tk in range(2 * u + 2):
                tile = s[i * BLK : (i + 1) * BLK, tk * BLK : (tk + 1) * BLK]
                if tk > t:
                    tile = jnp.full_like(tile, NEG)
                elif own and tk == t:
                    tile = jnp.where(below, tile, NEG)
                else:
                    seen = (doc_own if own else doc_oth)[tk] == doc_own[t]
                    if tk == t:
                        seen = seen & (lead == 1)
                    tile = tile + jnp.where(seen, 0.0, NEG)
                wide.append(tile)
            tall.append(jnp.concatenate(wide, axis=1))
        return jnp.concatenate(tall, axis=0)

    for u in reversed(range(N_CC // 2)):
        n = QB * (u + 1)
        first = u == N_CC // 2 - 1
        q = q_all[u * QB : (u + 1) * QB]
        g = g_all[u * QB : (u + 1) * QB]
        s1 = masked(dot_nt(q, k_own[:n]), u, True)
        s2 = masked(dot_nt(q, k_oth[:n]), u, False)
        top = jnp.maximum(
            jnp.max(s1, axis=1, keepdims=True), jnp.max(s2, axis=1, keepdims=True)
        )
        e1 = jnp.exp2((s1 - top) * (SCALE * LOG2E))
        e2 = jnp.exp2((s2 - top) * (SCALE * LOG2E))
        total = jnp.sum(e1, axis=1, keepdims=True) + jnp.sum(e2, axis=1, keepdims=True)
        inv = 1.0 / total
        p1, p2 = e1 * inv, e2 * inv
        b1, b2 = p1.astype(jnp.bfloat16), p2.astype(jnp.bfloat16)
        out = (dot_nn(b1, v_own[:n]) + dot_nn(b2, v_oth[:n])).astype(jnp.bfloat16)
        delta = jnp.sum(g.astype(jnp.float32) * out.astype(jnp.float32), axis=1, keepdims=True)
        d1 = (p1 * (dot_nt(g, v_own[:n]) - delta)).astype(jnp.bfloat16)
        d2 = (p2 * (dot_nt(g, v_oth[:n]) - delta)).astype(jnp.bfloat16)
        dq = ((dot_nn(d1, k_own[:n]) + dot_nn(d2, k_oth[:n])) * SCALE).astype(jnp.bfloat16)
        for i in range(2):
            at = pl.ds(slot(2 * u + i), N_Y)
            part = slice(i * BLK, (i + 1) * BLK)
            outdq_ref[at, 0] = out[part].reshape(N_Y, ROWS, HD)
            outdq_ref[at, 1] = dq[part].reshape(N_Y, ROWS, HD)
        q_t, g_t = q.T, g.T
        for index, left, right in ((0, q_t, d1), (1, g_t, b1), (2, q_t, d2), (3, g_t, b2)):
            new = dot_nn(left, right)
            acc[index, :, :n] = new if first else acc[index, :, :n] + new

    for t in range(N_CC):
        at = pl.ds(slot(t), N_Y)
        cols = slice(t * BLK, (t + 1) * BLK)
        own_ref[at, 0] = (acc[0, :, cols] * SCALE).T.reshape(N_Y, ROWS, HD)
        own_ref[at, 1] = acc[1, :, cols].T.reshape(N_Y, ROWS, HD)
        sent_ref[at, 0] = (acc[2, :, cols] * SCALE).T.astype(jnp.bfloat16).reshape(N_Y, ROWS, HD)
        sent_ref[at, 1] = acc[3, :, cols].T.astype(jnp.bfloat16).reshape(N_Y, ROWS, HD)


def whole(space=VM):
    return pl.BlockSpec(memory_space=space)


def shape(*dims, kind=jnp.bfloat16):
    return jax.ShapeDtypeStruct(dims, kind)


def per_device(queries, keys, values, grad_out, block_doc):
    packed = pl.pallas_call(
        pack_kernel,
        name="pack",
        out_shape=shape(GRP, 4, ROWS, HD),
        in_specs=[whole()] * 4,
        out_specs=whole(),
    )(keys, values, queries, grad_out)
    mine = lax.all_to_all(packed, ("cc", "y"), 0, 0, tiled=True)
    swap = [(0, 1), (1, 0)]
    other = lax.ppermute(mine[:, 0:2], "core", swap)
    ids = jnp.stack([lax.axis_index("xh"), lax.axis_index("core")]).astype(jnp.int32)
    half_rows = N_CC * BLK
    outdq, own, sent = pl.pallas_call(
        attention_kernel,
        name="attention",
        out_shape=(
            shape(GRP, 2, ROWS, HD),
            shape(GRP, 2, ROWS, HD, kind=jnp.float32),
            shape(GRP, 2, ROWS, HD),
        ),
        in_specs=[whole(pltpu.SMEM), whole(pltpu.SMEM), whole(), whole()],
        out_specs=(whole(), whole(), whole()),
        scratch_shapes=[VM((half_rows, HD), jnp.bfloat16)] * 6
        + [VM((4, HD, half_rows), jnp.float32)],
    )(ids, block_doc, mine, other)
    received = lax.ppermute(sent, "core", swap)
    back = pl.pallas_call(
        combine_kernel,
        name="combine",
        out_shape=shape(GRP, 4, ROWS, HD),
        in_specs=[whole()] * 3,
        out_specs=whole(),
    )(outdq, own, received)
    back = lax.all_to_all(back, ("cc", "y"), 0, 0, tiled=True)
    return tuple(
        pl.pallas_call(
            unpack_kernel,
            name="unpack",
            out_shape=(shape(ROWS, GRP * HD),) * 4,
            in_specs=[whole()],
            out_specs=(whole(),) * 4,
        )(back)
    )


def solution(mesh):
    split = Mesh(mesh.devices.reshape(N_CC, 2, 2, N_Y), ("cc", "core", "xh", "y"))
    rows = P(("cc", "core", "xh", "y"), None)
    return jax.shard_map(
        per_device,
        mesh=split,
        in_specs=(rows, rows, rows, rows, P()),
        out_specs=(rows,) * 4,
        check_vma=False,
    )
```

```python
import functools

import jax
import jax.numpy as jnp
from jax import lax
from jax.experimental import pallas as pl
from jax.experimental.pallas import tpu as pltpu
from jax.sharding import Mesh, PartitionSpec as P

HD = 128
BLK = 128
SCALE = HD ** (-0.5)
LOG2E = 1.4426950408889634
NEG = -1e30

N_CC = 8
N_Y = 4
GRP = N_CC * N_Y
ROWS = 32
QB = 256
VM = pltpu.VMEM


def pack_kernel(k_ref, v_ref, q_ref, g_ref, o_ref, buf, sems):
    copies = [
        pltpu.make_async_copy(ref, buf.at[a], sems.at[a])
        for a, ref in enumerate((k_ref, v_ref, q_ref, g_ref))
    ]
    for copy in copies:
        copy.start()
    for a, copy in enumerate(copies):
        copy.wait()
        for h in range(GRP):
            o_ref[h, a] = buf[a, :, h * HD : (h + 1) * HD]


def unpack_kernel(x_ref, o0_ref, o1_ref, o2_ref, o3_ref, buf, sems):
    copies = [
        pltpu.make_async_copy(buf.at[a], ref, sems.at[a])
        for a, ref in enumerate((o0_ref, o1_ref, o2_ref, o3_ref))
    ]
    for a, copy in enumerate(copies):
        for h in range(GRP):
            buf[a, :, h * HD : (h + 1) * HD] = x_ref[h, a]
        copy.start()
    for copy in copies:
        copy.wait()


def combine_kernel(outdq_ref, own_ref, recv_ref, o_ref):
    o_ref[:, 0:2] = outdq_ref[...]
    o_ref[:, 2:4] = (own_ref[...] + recv_ref[...].astype(jnp.float32)).astype(jnp.bfloat16)


def dot_nt(a, b):
    return lax.dot_general(a, b, (((1,), (1,)), ((), ())), preferred_element_type=jnp.float32)


def dot_nn(a, b):
    return lax.dot_general(a, b, (((1,), (0,)), ((), ())), preferred_element_type=jnp.float32)


def attention_kernel(
    doc_ref, x_ref, oth_ref,
    outdq_ref, own_ref, sent_ref,
    k_own, v_own, k_oth, v_oth, q_all, g_all, acc,
):
    half, core = lax.axis_index("xh"), lax.axis_index("core")
    lead = jnp.where(half == core, 0, 1)

    def slot(t):
        return jnp.where(half == 1, N_CC - 1 - t, t) * N_Y

    for t in range(N_CC):
        rows = slice(t * BLK, (t + 1) * BLK)
        at = pl.ds(slot(t), N_Y)
        k_own[rows] = x_ref[at, 0].reshape(BLK, HD)
        v_own[rows] = x_ref[at, 1].reshape(BLK, HD)
        q_all[rows] = x_ref[at, 2].reshape(BLK, HD)
        g_all[rows] = x_ref[at, 3].reshape(BLK, HD)
        k_oth[rows] = oth_ref[at, 0].reshape(BLK, HD)
        v_oth[rows] = oth_ref[at, 1].reshape(BLK, HD)

    doc_own = [doc_ref[half * 16 + 2 * t + lead] for t in range(N_CC)]
    doc_oth = [doc_ref[half * 16 + 2 * t + 1 - lead] for t in range(N_CC)]

    row = lax.broadcasted_iota(jnp.int32, (BLK, BLK), 0)
    col = lax.broadcasted_iota(jnp.int32, (BLK, BLK), 1)
    below = col <= row

    def masked(s, u, own):
        tall = []
        for i in range(2):
            t = 2 * u + i
            wide = []
            for tk in range(2 * u + 2):
                tile = s[i * BLK : (i + 1) * BLK, tk * BLK : (tk + 1) * BLK]
                if tk > t:
                    tile = jnp.full_like(tile, NEG)
                elif own and tk == t:
                    tile = jnp.where(below, tile, NEG)
                else:
                    seen = (doc_own if own else doc_oth)[tk] == doc_own[t]
                    if tk == t:
                        seen = seen & (lead == 1)
                    tile = tile + jnp.where(seen, 0.0, NEG)
                wide.append(tile)
            tall.append(jnp.concatenate(wide, axis=1))
        return jnp.concatenate(tall, axis=0)

    for u in reversed(range(N_CC // 2)):
        n = QB * (u + 1)
        first = u == N_CC // 2 - 1
        q = q_all[u * QB : (u + 1) * QB]
        g = g_all[u * QB : (u + 1) * QB]
        s1 = masked(dot_nt(q, k_own[:n]), u, True)
        s2 = masked(dot_nt(q, k_oth[:n]), u, False)
        top = jnp.maximum(
            jnp.max(s1, axis=1, keepdims=True), jnp.max(s2, axis=1, keepdims=True)
        )
        e1 = jnp.exp2((s1 - top) * (SCALE * LOG2E))
        e2 = jnp.exp2((s2 - top) * (SCALE * LOG2E))
        total = jnp.sum(e1, axis=1, keepdims=True) + jnp.sum(e2, axis=1, keepdims=True)
        inv = 1.0 / total
        p1, p2 = e1 * inv, e2 * inv
        b1, b2 = p1.astype(jnp.bfloat16), p2.astype(jnp.bfloat16)
        out = (dot_nn(b1, v_own[:n]) + dot_nn(b2, v_oth[:n])).astype(jnp.bfloat16)
        delta = jnp.sum(g.astype(jnp.float32) * out.astype(jnp.float32), axis=1, keepdims=True)
        d1 = (p1 * (dot_nt(g, v_own[:n]) - delta)).astype(jnp.bfloat16)
        d2 = (p2 * (dot_nt(g, v_oth[:n]) - delta)).astype(jnp.bfloat16)
        dq = ((dot_nn(d1, k_own[:n]) + dot_nn(d2, k_oth[:n])) * SCALE).astype(jnp.bfloat16)
        for i in range(2):
            at = pl.ds(slot(2 * u + i), N_Y)
            part = slice(i * BLK, (i + 1) * BLK)
            outdq_ref[at, 0] = out[part].reshape(N_Y, ROWS, HD)
            outdq_ref[at, 1] = dq[part].reshape(N_Y, ROWS, HD)
        q_t, g_t = q.T, g.T
        for index, left, right in ((0, q_t, d1), (1, g_t, b1), (2, q_t, d2), (3, g_t, b2)):
            new = dot_nn(left, right)
            acc[index, :, :n] = new if first else acc[index, :, :n] + new

    for t in range(N_CC):
        at = pl.ds(slot(t), N_Y)
        cols = slice(t * BLK, (t + 1) * BLK)
        own_ref[at, 0] = (acc[0, :, cols] * SCALE).T.reshape(N_Y, ROWS, HD)
        own_ref[at, 1] = acc[1, :, cols].T.reshape(N_Y, ROWS, HD)
        sent_ref[at, 0] = (acc[2, :, cols] * SCALE).T.astype(jnp.bfloat16).reshape(N_Y, ROWS, HD)
        sent_ref[at, 1] = acc[3, :, cols].T.astype(jnp.bfloat16).reshape(N_Y, ROWS, HD)


def whole(space=VM):
    return pl.BlockSpec(memory_space=space)


def shape(*dims, kind=jnp.bfloat16):
    return jax.ShapeDtypeStruct(dims, kind)


def near(*dims, kind=jnp.bfloat16):
    return VM(dims, kind)


def far(x):
    return pltpu.with_memory_space_constraint(x, pltpu.HBM)


def grant(mib):
    return pltpu.CompilerParams(vmem_limit_bytes=mib << 20)


def staging():
    return [VM((4, ROWS, GRP * HD), jnp.bfloat16), pltpu.SemaphoreType.DMA((4,))]


def held(x):
    return pltpu.with_memory_space_constraint(x, VM)


def per_device(queries, keys, values, grad_out, block_doc):
    packed = pl.pallas_call(
        pack_kernel,
        name="pack",
        compiler_params=grant(8),
        out_shape=near(GRP, 4, ROWS, HD),
        in_specs=[whole(pltpu.HBM)] * 4,
        out_specs=whole(),
        scratch_shapes=staging(),
    )(*[far(x) for x in (keys, values, queries, grad_out)])
    mine = lax.all_to_all(packed, ("cc", "y"), 0, 0, tiled=True)
    swap = [(0, 1), (1, 0)]
    other = lax.ppermute(mine[:, 0:2], "core", swap)
    half_rows = N_CC * BLK
    outdq, own, sent = pl.pallas_call(
        attention_kernel,
        name="attention",
        compiler_params=grant(40),
        out_shape=(
            near(GRP, 2, ROWS, HD),
            near(GRP, 2, ROWS, HD, kind=jnp.float32),
            near(GRP, 2, ROWS, HD),
        ),
        in_specs=[whole(pltpu.SMEM), whole(), whole()],
        out_specs=(whole(), whole(), whole()),
        scratch_shapes=[VM((half_rows, HD), jnp.bfloat16)] * 6
        + [VM((4, HD, half_rows), jnp.float32)],
    )(block_doc, held(mine), held(other))
    received = lax.ppermute(sent, "core", swap)
    back = pl.pallas_call(
        combine_kernel,
        name="combine",
        compiler_params=grant(8),
        out_shape=near(GRP, 4, ROWS, HD),
        in_specs=[whole()] * 3,
        out_specs=whole(),
    )(held(outdq), held(own), held(received))
    back = lax.all_to_all(back, ("cc", "y"), 0, 0, tiled=True)
    return tuple(
        pl.pallas_call(
            unpack_kernel,
            name="unpack",
            compiler_params=grant(8),
            out_shape=(shape(ROWS, GRP * HD),) * 4,
            in_specs=[whole()],
            out_specs=(whole(pltpu.HBM),) * 4,
            scratch_shapes=staging(),
        )(held(back))
    )


def solution(mesh):
    split = Mesh(mesh.devices.reshape(N_CC, 2, 2, N_Y), ("cc", "core", "xh", "y"))
    rows = P(("cc", "core", "xh", "y"), None)
    return jax.shard_map(
        per_device,
        mesh=split,
        in_specs=(rows, rows, rows, rows, P()),
        out_specs=(rows,) * 4,
        check_vma=False,
    )
```

```python
import functools

import jax
import jax.numpy as jnp
from jax import lax
from jax.experimental import pallas as pl
from jax.experimental.pallas import tpu as pltpu
from jax.sharding import Mesh, PartitionSpec as P

HD = 128
BLK = 128
SCALE = HD ** (-0.5)
LOG2E = 1.4426950408889634
NEG = -1e30

N_CC = 8
N_Y = 4
GRP = N_CC * N_Y
ROWS = 32
QB = 256
RC = 64
VM = pltpu.VMEM


def pack_kernel(k_ref, v_ref, q_ref, g_ref, o_ref, buf, sems):
    copies = [
        pltpu.make_async_copy(ref, buf.at[a], sems.at[a])
        for a, ref in enumerate((k_ref, v_ref, q_ref, g_ref))
    ]
    for copy in copies:
        copy.start()
    for a, copy in enumerate(copies):
        copy.wait()
        for h in range(GRP):
            o_ref[h, a] = buf[a, :, h * HD : (h + 1) * HD]


def unpack_kernel(x_ref, o0_ref, o1_ref, o2_ref, o3_ref, buf, sems):
    copies = [
        pltpu.make_async_copy(buf.at[a], ref, sems.at[a])
        for a, ref in enumerate((o0_ref, o1_ref, o2_ref, o3_ref))
    ]
    for a, copy in enumerate(copies):
        for h in range(GRP):
            buf[a, :, h * HD : (h + 1) * HD] = x_ref[h, a]
        copy.start()
    for copy in copies:
        copy.wait()


def dot_nt(a, b):
    return lax.dot_general(a, b, (((1,), (1,)), ((), ())), preferred_element_type=jnp.float32)


def dot_nn(a, b):
    return lax.dot_general(a, b, (((1,), (0,)), ((), ())), preferred_element_type=jnp.float32)


def placed():
    half, core = lax.axis_index("xh"), lax.axis_index("core")
    lead = jnp.where(half == core, 0, 1)
    slots = [jnp.where(half == 1, N_CC - 1 - t, t) for t in range(N_CC)]
    return half, lead, slots


def masked(s, u, bias):
    tall = []
    for i in range(2):
        wide = [
            bias(2 * u + i, tk, s[i * BLK : (i + 1) * BLK, tk * BLK : (tk + 1) * BLK])
            for tk in range(2 * u + 2)
        ]
        tall.append(jnp.concatenate(wide, axis=1))
    return jnp.concatenate(tall, axis=0)


def rows_of(u):
    return slice(u * QB, (u + 1) * QB)


def chunks(u):
    return [(low, slice(u * QB + low, u * QB + low + RC)) for low in range(0, QB, RC)]


def joined(parts):
    return [jnp.concatenate(column, axis=0) for column in zip(*parts)]


def own_kernel(doc_ref, x_ref, all_ref, e_ref, w_ref, m_ref, l_ref):
    half, lead, slots = placed()
    for t in range(N_CC):
        for a in range(4):
            all_ref[a, t * BLK : (t + 1) * BLK] = x_ref[:, slots[t], a].reshape(BLK, HD)
    doc = [doc_ref[half * 16 + 2 * t + lead] for t in range(N_CC)]
    below = lax.broadcasted_iota(jnp.int32, (BLK, BLK), 1) <= lax.broadcasted_iota(
        jnp.int32, (BLK, BLK), 0
    )

    def bias(t, tk, tile):
        if tk > t:
            return jnp.full_like(tile, NEG)
        if tk == t:
            return jnp.where(below, tile, NEG)
        return tile + jnp.where(doc[tk] == doc[t], 0.0, NEG)

    for u in reversed(range(N_CC // 2)):
        n, r = QB * (u + 1), rows_of(u)
        s = masked(dot_nt(all_ref[2, r], all_ref[0, :n]), u, bias)
        w_ref[r, :n] = dot_nt(all_ref[3, r], all_ref[1, :n])
        for low, part in chunks(u):
            piece = s[low : low + RC]
            top = jnp.max(piece, axis=1, keepdims=True)
            e = jnp.exp2((piece - top) * (SCALE * LOG2E))
            e_ref[part, :n] = e
            m_ref[part] = jnp.broadcast_to(top, (RC, HD))
            l_ref[part] = jnp.broadcast_to(jnp.sum(e, axis=1, keepdims=True), (RC, HD))


def other_kernel(
    doc_ref, all_ref, oth_ref, e_ref, w_ref, m_ref, l_ref,
    out_ref, sent_ref, b_ref, d_ref, k_ref, v_oth, acc,
):
    half, lead, slots = placed()
    for t in range(N_CC):
        k_ref[t * BLK : (t + 1) * BLK] = oth_ref[:, slots[t], 0].reshape(BLK, HD)
        v_oth[t * BLK : (t + 1) * BLK] = oth_ref[:, slots[t], 1].reshape(BLK, HD)
    doc_own = [doc_ref[half * 16 + 2 * t + lead] for t in range(N_CC)]
    doc_oth = [doc_ref[half * 16 + 2 * t + 1 - lead] for t in range(N_CC)]

    def bias(t, tk, tile):
        if tk > t:
            return jnp.full_like(tile, NEG)
        seen = doc_oth[tk] == doc_own[t]
        if tk == t:
            seen = seen & (lead == 1)
        return tile + jnp.where(seen, 0.0, NEG)

    last = N_CC // 2 - 1

    def scores(u):
        n, r = QB * (u + 1), rows_of(u)
        return dot_nt(all_ref[2, r], k_ref[:n]), dot_nt(all_ref[3, r], v_oth[:n])

    def softmax(u, s):
        n = QB * (u + 1)
        s = masked(s, u, bias)
        parts = []
        for low, part in chunks(u):
            piece = s[low : low + RC]
            m_own = m_ref[part, :1]
            top = jnp.maximum(m_own, jnp.max(piece, axis=1, keepdims=True))
            e = jnp.exp2((piece - top) * (SCALE * LOG2E))
            fade = jnp.exp2((m_own - top) * (SCALE * LOG2E))
            inv = 1.0 / (l_ref[part, :1] * fade + jnp.sum(e, axis=1, keepdims=True))
            p1, p2 = e_ref[part, :n] * (fade * inv), e * inv
            parts.append((p1, p2, p1.astype(jnp.bfloat16), p2.astype(jnp.bfloat16)))
        p1, p2, b1, b2 = joined(parts)
        b_ref[rows_of(u), :n] = b1
        return p1, p2, b1, b2

    def output(u, b1, b2):
        n = QB * (u + 1)
        out = (dot_nn(b1, all_ref[1, :n]) + dot_nn(b2, v_oth[:n])).astype(jnp.bfloat16)
        for i in range(2):
            out_ref[:, slots[2 * u + i]] = out[i * BLK : (i + 1) * BLK].reshape(N_Y, ROWS, HD)
        return out

    def score_grads(u, p1, p2, w, out):
        n = QB * (u + 1)
        parts = []
        for low, part in chunks(u):
            some = slice(low, low + RC)
            g = all_ref[3, part].astype(jnp.float32)
            delta = jnp.sum(g * out[some].astype(jnp.float32), axis=1, keepdims=True)
            d2 = (p2[some] * (w[some] - delta)).astype(jnp.bfloat16)
            d_ref[0, part, :n] = (p1[some] * (w_ref[part, :n] - delta)).astype(jnp.bfloat16)
            d_ref[1, part, :n] = d2
            parts.append((d2,))
        return joined(parts)[0]

    def key_grads(u, d2, b2):
        n, r = QB * (u + 1), rows_of(u)
        for a, left, right in ((0, all_ref[2, r].T, d2), (1, all_ref[3, r].T, b2)):
            new = dot_nn(left, right)
            if u < last:
                new = acc[a, :, :n] + new
            if u:
                acc[a, :, : n - QB] = new[:, : n - QB]
            done = (new[:, n - QB :] * (1.0 if a else SCALE)).astype(jnp.bfloat16).T
            for i in range(2):
                part = done[i * BLK : (i + 1) * BLK].reshape(N_Y, ROWS, HD)
                sent_ref[:, slots[2 * u + i], a] = part

    ready = scores(last)
    before = None
    for u in reversed(range(-1, last + 1)):
        s, w = ready
        if u > 0:
            ready = scores(u - 1)
        if before is not None:
            p1, p2, b2, w_b, out = before
            d2 = score_grads(u + 1, p1, p2, w_b, out)
        if u >= 0:
            q1, q2, c1, c2 = softmax(u, s)
        if before is not None:
            key_grads(u + 1, d2, b2)
        if u >= 0:
            before = q1, q2, c2, w, output(u, c1, c2)


def rest_kernel(all_ref, k_ref, b_ref, d_ref, dq_ref, own_ref):
    _, _, slots = placed()
    q_t, g_t = all_ref[2].T, all_ref[3].T
    for u in reversed(range(N_CC // 2)):
        n, r = QB * (u + 1), rows_of(u)
        dq = dot_nn(d_ref[0, r, :n], all_ref[0, :n]) + dot_nn(d_ref[1, r, :n], k_ref[:n])
        dq = (dq * SCALE).astype(jnp.bfloat16)
        low = u * QB
        dk = dot_nn(q_t[:, low:], d_ref[0, low:, r]) * SCALE
        dv = dot_nn(g_t[:, low:], b_ref[low:, r])
        for i in range(2):
            at, part = slots[2 * u + i], slice(i * BLK, (i + 1) * BLK)
            dq_ref[:, at] = dq[part].reshape(N_Y, ROWS, HD)
            own_ref[:, at, 0] = dk[:, part].T.reshape(N_Y, ROWS, HD)
            own_ref[:, at, 1] = dv[:, part].T.reshape(N_Y, ROWS, HD)


def combine_kernel(out_ref, dq_ref, own_ref, recv_ref, o_ref):
    o_ref[:, :, 0] = out_ref[...]
    o_ref[:, :, 1] = dq_ref[...]
    o_ref[:, :, 2:4] = (own_ref[...] + recv_ref[...].astype(jnp.float32)).astype(jnp.bfloat16)


def whole(space=VM):
    return pl.BlockSpec(memory_space=space)


def shape(*dims, kind=jnp.bfloat16):
    return jax.ShapeDtypeStruct(dims, kind)


def near(*dims, kind=jnp.bfloat16):
    return VM(dims, kind)


def far(x):
    return pltpu.with_memory_space_constraint(x, pltpu.HBM)


def grant(mib):
    return pltpu.CompilerParams(vmem_limit_bytes=mib << 20)


def staging():
    return [VM((4, ROWS, GRP * HD), jnp.bfloat16), pltpu.SemaphoreType.DMA((4,))]


def held(x):
    return pltpu.with_memory_space_constraint(x, VM)


def per_device(queries, keys, values, grad_out, block_doc):
    packed = pl.pallas_call(
        pack_kernel,
        name="pack",
        compiler_params=grant(8),
        out_shape=near(GRP, 4, ROWS, HD),
        in_specs=[whole(pltpu.HBM)] * 4,
        out_specs=whole(),
        scratch_shapes=staging(),
    )(*[far(x) for x in (keys, values, queries, grad_out)])
    mine = lax.all_to_all(packed, ("y", "cc"), 0, 0, tiled=True)
    swap = [(0, 1), (1, 0)]
    mine = mine.reshape(N_Y, N_CC, 4, ROWS, HD)
    other = lax.ppermute(mine[:, :, 0:2], "core", swap)
    smem = whole(pltpu.SMEM)
    full = N_CC * BLK
    f32 = jnp.float32
    everything, exps, weights, top, total = pl.pallas_call(
        own_kernel,
        name="own_keys",
        compiler_params=grant(16),
        out_shape=(
            near(4, full, HD),
            near(full, full, kind=f32),
            near(full, full, kind=f32),
            near(full, HD, kind=f32),
            near(full, HD, kind=f32),
        ),
        in_specs=[smem, whole()],
        out_specs=(whole(),) * 5,
    )(block_doc, held(mine))
    out, sent, probs, grads, k_other = pl.pallas_call(
        other_kernel,
        name="other_keys",
        compiler_params=grant(24),
        out_shape=(
            near(N_Y, N_CC, ROWS, HD),
            near(N_Y, N_CC, 2, ROWS, HD),
            near(full, full),
            near(2, full, full),
            near(full, HD),
        ),
        in_specs=[smem] + [whole()] * 6,
        out_specs=(whole(),) * 5,
        scratch_shapes=[VM((full, HD), jnp.bfloat16), VM((2, HD, full), f32)],
    )(block_doc, *[held(x) for x in (everything, other, exps, weights, top, total)])
    received = lax.ppermute(sent, "core", swap)
    dq, own = pl.pallas_call(
        rest_kernel,
        name="rest",
        compiler_params=grant(16),
        out_shape=(near(N_Y, N_CC, ROWS, HD), near(N_Y, N_CC, 2, ROWS, HD, kind=f32)),
        in_specs=[whole()] * 4,
        out_specs=(whole(),) * 2,
    )(*[held(x) for x in (everything, k_other, probs, grads)])
    back = pl.pallas_call(
        combine_kernel,
        name="combine",
        compiler_params=grant(8),
        out_shape=near(N_Y, N_CC, 4, ROWS, HD),
        in_specs=[whole()] * 4,
        out_specs=whole(),
    )(held(out), held(dq), held(own), held(received))
    back = lax.all_to_all(back.reshape(GRP, 4, ROWS, HD), ("y", "cc"), 0, 0, tiled=True)
    return tuple(
        pl.pallas_call(
            unpack_kernel,
            name="unpack",
            compiler_params=grant(8),
            out_shape=(shape(ROWS, GRP * HD),) * 4,
            in_specs=[whole()],
            out_specs=(whole(pltpu.HBM),) * 4,
            scratch_shapes=staging(),
        )(held(back))
    )


def solution(mesh):
    split = Mesh(mesh.devices.reshape(N_CC, 2, 2, N_Y), ("cc", "core", "xh", "y"))
    rows = P(("cc", "core", "xh", "y"), None)
    return jax.shard_map(
        per_device,
        mesh=split,
        in_specs=(rows, rows, rows, rows, P()),
        out_specs=(rows,) * 4,
        check_vma=False,
    )
```

```python
import functools

import jax
import jax.numpy as jnp
from jax import lax
from jax.experimental import pallas as pl
from jax.experimental.pallas import tpu as pltpu
from jax.sharding import Mesh, PartitionSpec as P

HD = 128
BLK = 128
SCALE = HD ** (-0.5)
LOG2E = 1.4426950408889634
NEG = -1e30

N_CC = 8
N_Y = 4
GRP = N_CC * N_Y
ROWS = 32
QB = 256
RC = 256
VM = pltpu.VMEM


def pack_kernel(k_ref, v_ref, q_ref, g_ref, o_ref, buf, sems):
    copies = [
        pltpu.make_async_copy(ref, buf.at[a], sems.at[a])
        for a, ref in enumerate((k_ref, v_ref, q_ref, g_ref))
    ]
    for copy in copies:
        copy.start()
    for a, copy in enumerate(copies):
        copy.wait()
        for h in range(GRP):
            o_ref[h, a] = buf[a, :, h * HD : (h + 1) * HD]


def unpack_kernel(x_ref, o0_ref, o1_ref, o2_ref, o3_ref, buf, sems):
    copies = [
        pltpu.make_async_copy(buf.at[a], ref, sems.at[a])
        for a, ref in enumerate((o0_ref, o1_ref, o2_ref, o3_ref))
    ]
    for a, copy in enumerate(copies):
        for h in range(GRP):
            buf[a, :, h * HD : (h + 1) * HD] = x_ref[h, a]
        copy.start()
    for copy in copies:
        copy.wait()


def dot_nt(a, b):
    return lax.dot_general(a, b, (((1,), (1,)), ((), ())), preferred_element_type=jnp.float32)


def dot_nn(a, b):
    return lax.dot_general(a, b, (((1,), (0,)), ((), ())), preferred_element_type=jnp.float32)


def placed():
    half, core = lax.axis_index("xh"), lax.axis_index("core")
    lead = jnp.where(half == core, 0, 1)
    slots = [jnp.where(half == 1, N_CC - 1 - t, t) for t in range(N_CC)]
    return half, lead, slots


def masked(s, u, bias):
    tall = []
    for i in range(2):
        wide = [
            bias(2 * u + i, tk, s[i * BLK : (i + 1) * BLK, tk * BLK : (tk + 1) * BLK])
            for tk in range(2 * u + 2)
        ]
        tall.append(jnp.concatenate(wide, axis=1))
    return jnp.concatenate(tall, axis=0)


def rows_of(u):
    return slice(u * QB, (u + 1) * QB)


def chunks(u):
    return [(low, slice(u * QB + low, u * QB + low + RC)) for low in range(0, QB, RC)]


def joined(parts):
    return [jnp.concatenate(column, axis=0) for column in zip(*parts)]


def own_kernel(doc_ref, x_ref, all_ref, e_ref, w_ref, m_ref, l_ref):
    half, lead, slots = placed()
    for t in range(N_CC):
        for a in range(4):
            all_ref[a, t * BLK : (t + 1) * BLK] = x_ref[:, slots[t], a].reshape(BLK, HD)
    doc = [doc_ref[half * 16 + 2 * t + lead] for t in range(N_CC)]
    below = lax.broadcasted_iota(jnp.int32, (BLK, BLK), 1) <= lax.broadcasted_iota(
        jnp.int32, (BLK, BLK), 0
    )

    def bias(t, tk, tile):
        if tk > t:
            return jnp.full_like(tile, NEG)
        if tk == t:
            return jnp.where(below, tile, NEG)
        return tile + jnp.where(doc[tk] == doc[t], 0.0, NEG)

    for u in reversed(range(N_CC // 2)):
        n, r = QB * (u + 1), rows_of(u)
        s = masked(dot_nt(all_ref[2, r], all_ref[0, :n]), u, bias)
        w_ref[r, :n] = dot_nt(all_ref[3, r], all_ref[1, :n])
        for low, part in chunks(u):
            piece = s[low : low + RC]
            top = jnp.max(piece, axis=1, keepdims=True)
            e = jnp.exp2((piece - top) * (SCALE * LOG2E))
            e_ref[part, :n] = e
            m_ref[part] = jnp.broadcast_to(top, (RC, HD))
            l_ref[part] = jnp.broadcast_to(jnp.sum(e, axis=1, keepdims=True), (RC, HD))


def other_kernel(
    doc_ref, all_ref, oth_ref, e_ref, m_ref, l_ref,
    out_ref, sent_ref, b_ref, d_ref, k_ref, f_ref, delta_ref, v_oth, acc,
):
    half, lead, slots = placed()
    for t in range(N_CC):
        k_ref[t * BLK : (t + 1) * BLK] = oth_ref[:, slots[t], 0].reshape(BLK, HD)
        v_oth[t * BLK : (t + 1) * BLK] = oth_ref[:, slots[t], 1].reshape(BLK, HD)
    doc_own = [doc_ref[half * 16 + 2 * t + lead] for t in range(N_CC)]
    doc_oth = [doc_ref[half * 16 + 2 * t + 1 - lead] for t in range(N_CC)]

    def bias(t, tk, tile):
        if tk > t:
            return jnp.full_like(tile, NEG)
        seen = doc_oth[tk] == doc_own[t]
        if tk == t:
            seen = seen & (lead == 1)
        return tile + jnp.where(seen, 0.0, NEG)

    last = N_CC // 2 - 1

    def scores(u):
        n, r = QB * (u + 1), rows_of(u)
        return dot_nt(all_ref[2, r], k_ref[:n])

    def weights(u):
        return dot_nt(all_ref[3, rows_of(u)], v_oth[: QB * (u + 1)])

    def softmax(u, s):
        n = QB * (u + 1)
        s = masked(s, u, bias)
        parts = []
        for low, part in chunks(u):
            piece = s[low : low + RC]
            m_own = m_ref[part, :1]
            top = jnp.maximum(m_own, jnp.max(piece, axis=1, keepdims=True))
            e = jnp.exp2((piece - top) * (SCALE * LOG2E))
            fade = jnp.exp2((m_own - top) * (SCALE * LOG2E))
            inv = 1.0 / (l_ref[part, :1] * fade + jnp.sum(e, axis=1, keepdims=True))
            fade = fade * inv
            f_ref[part] = jnp.broadcast_to(fade, (RC, HD))
            b1, p2 = (e_ref[part, :n] * fade).astype(jnp.bfloat16), e * inv
            parts.append((p2, b1, p2.astype(jnp.bfloat16)))
        p2, b1, b2 = joined(parts)
        b_ref[rows_of(u), :n] = b1
        return p2, b1, b2

    def output(u, b1, b2):
        n = QB * (u + 1)
        out = (dot_nn(b1, all_ref[1, :n]) + dot_nn(b2, v_oth[:n])).astype(jnp.bfloat16)
        for i in range(2):
            out_ref[:, slots[2 * u + i]] = out[i * BLK : (i + 1) * BLK].reshape(N_Y, ROWS, HD)
        return out

    def score_grads(u, p2, w, out):
        n = QB * (u + 1)
        parts = []
        for low, part in chunks(u):
            some = slice(low, low + RC)
            g = all_ref[3, part].astype(jnp.float32)
            delta = jnp.sum(g * out[some].astype(jnp.float32), axis=1, keepdims=True)
            delta_ref[part] = jnp.broadcast_to(delta, (RC, HD))
            parts.append(((p2[some] * (w[some] - delta)).astype(jnp.bfloat16),))
        d2 = joined(parts)[0]
        d_ref[rows_of(u), :n] = d2
        return d2

    def key_grads(u, a, right):
        n, r = QB * (u + 1), rows_of(u)
        new = dot_nn(all_ref[2 + a, r].T, right)
        if u < last:
            new = acc[a, :, :n] + new
        if u:
            acc[a, :, : n - QB] = new[:, : n - QB]
        done = (new[:, n - QB :] * (1.0 if a else SCALE)).astype(jnp.bfloat16).T
        for i in range(2):
            part = done[i * BLK : (i + 1) * BLK].reshape(N_Y, ROWS, HD)
            sent_ref[:, slots[2 * u + i], a] = part

    ready = scores(last)
    kept = {}
    for u in reversed(range(last + 1)):
        s = ready
        if u:
            ready = scores(u - 1)
        p2, b1, b2 = softmax(u, s)
        kept[u] = p2, output(u, b1, b2)
        key_grads(u, 1, b2)
    ready = weights(last)
    for u in reversed(range(last + 1)):
        w = ready
        if u:
            ready = weights(u - 1)
        p2, out = kept[u]
        key_grads(u, 0, score_grads(u, p2, w, out))


def rest_kernel(
    all_ref, k_ref, e_ref, w_ref, f_ref, delta_ref, b_ref, d_ref, dq_ref, own_ref, d_own
):
    _, _, slots = placed()
    q_t, g_t = all_ref[2].T, all_ref[3].T
    for u in reversed(range(N_CC // 2)):
        n, r = QB * (u + 1), rows_of(u)
        low = u * QB
        dv = dot_nn(g_t[:, low:], b_ref[low:, r])
        d = e_ref[r, :n] * f_ref[r, :1] * (w_ref[r, :n] - delta_ref[r, :1])
        d = d.astype(jnp.bfloat16)
        d_own[r, :n] = d
        dq = dot_nn(d_ref[r, :n], k_ref[:n]) + dot_nn(d, all_ref[0, :n])
        dq = (dq * SCALE).astype(jnp.bfloat16)
        dk = dot_nn(q_t[:, low:], d_own[low:, r]) * SCALE
        for i in range(2):
            at, part = slots[2 * u + i], slice(i * BLK, (i + 1) * BLK)
            dq_ref[:, at] = dq[part].reshape(N_Y, ROWS, HD)
            own_ref[:, at, 0] = dk[:, part].T.reshape(N_Y, ROWS, HD)
            own_ref[:, at, 1] = dv[:, part].T.reshape(N_Y, ROWS, HD)


def combine_kernel(out_ref, dq_ref, own_ref, recv_ref, o_ref):
    o_ref[:, :, 0] = out_ref[...]
    o_ref[:, :, 1] = dq_ref[...]
    o_ref[:, :, 2:4] = (own_ref[...] + recv_ref[...].astype(jnp.float32)).astype(jnp.bfloat16)


def whole(space=VM):
    return pl.BlockSpec(memory_space=space)


def shape(*dims, kind=jnp.bfloat16):
    return jax.ShapeDtypeStruct(dims, kind)


def near(*dims, kind=jnp.bfloat16):
    return VM(dims, kind)


def far(x):
    return pltpu.with_memory_space_constraint(x, pltpu.HBM)


def grant(mib):
    return pltpu.CompilerParams(vmem_limit_bytes=mib << 20)


def staging():
    return [VM((4, ROWS, GRP * HD), jnp.bfloat16), pltpu.SemaphoreType.DMA((4,))]


def held(x):
    return pltpu.with_memory_space_constraint(x, VM)


def per_device(queries, keys, values, grad_out, block_doc):
    packed = pl.pallas_call(
        pack_kernel,
        name="pack",
        compiler_params=grant(8),
        out_shape=near(GRP, 4, ROWS, HD),
        in_specs=[whole(pltpu.HBM)] * 4,
        out_specs=whole(),
        scratch_shapes=staging(),
    )(*[far(x) for x in (keys, values, queries, grad_out)])
    mine = lax.all_to_all(packed, ("y", "cc"), 0, 0, tiled=True)
    swap = [(0, 1), (1, 0)]
    mine = mine.reshape(N_Y, N_CC, 4, ROWS, HD)
    other = lax.ppermute(mine[:, :, 0:2], "core", swap)
    smem = whole(pltpu.SMEM)
    full = N_CC * BLK
    f32 = jnp.float32
    everything, exps, weights, top, total = pl.pallas_call(
        own_kernel,
        name="own_keys",
        compiler_params=grant(16),
        out_shape=(
            near(4, full, HD),
            near(full, full, kind=f32),
            near(full, full, kind=f32),
            near(full, HD, kind=f32),
            near(full, HD, kind=f32),
        ),
        in_specs=[smem, whole()],
        out_specs=(whole(),) * 5,
    )(block_doc, held(mine))
    out, sent, probs, grads, k_other, fade, delta = pl.pallas_call(
        other_kernel,
        name="other_keys",
        compiler_params=grant(24),
        out_shape=(
            near(N_Y, N_CC, ROWS, HD),
            near(N_Y, N_CC, 2, ROWS, HD),
            near(full, full),
            near(full, full),
            near(full, HD),
            near(full, HD, kind=f32),
            near(full, HD, kind=f32),
        ),
        in_specs=[smem] + [whole()] * 5,
        out_specs=(whole(),) * 7,
        scratch_shapes=[VM((full, HD), jnp.bfloat16), VM((2, HD, full), f32)],
    )(block_doc, *[held(x) for x in (everything, other, exps, top, total)])
    received = lax.ppermute(sent, "core", swap)
    dq, own = pl.pallas_call(
        rest_kernel,
        name="rest",
        compiler_params=grant(16),
        out_shape=(near(N_Y, N_CC, ROWS, HD), near(N_Y, N_CC, 2, ROWS, HD, kind=f32)),
        in_specs=[whole()] * 8,
        out_specs=(whole(),) * 2,
        scratch_shapes=[VM((full, full), jnp.bfloat16)],
    )(*[held(x) for x in (everything, k_other, exps, weights, fade, delta, probs, grads)])
    back = pl.pallas_call(
        combine_kernel,
        name="combine",
        compiler_params=grant(8),
        out_shape=near(N_Y, N_CC, 4, ROWS, HD),
        in_specs=[whole()] * 4,
        out_specs=whole(),
    )(held(out), held(dq), held(own), held(received))
    back = lax.all_to_all(back.reshape(GRP, 4, ROWS, HD), ("y", "cc"), 0, 0, tiled=True)
    return tuple(
        pl.pallas_call(
            unpack_kernel,
            name="unpack",
            compiler_params=grant(8),
            out_shape=(shape(ROWS, GRP * HD),) * 4,
            in_specs=[whole()],
            out_specs=(whole(pltpu.HBM),) * 4,
            scratch_shapes=staging(),
        )(held(back))
    )


def solution(mesh):
    split = Mesh(mesh.devices.reshape(N_CC, 2, 2, N_Y), ("cc", "core", "xh", "y"))
    rows = P(("cc", "core", "xh", "y"), None)
    return jax.shard_map(
        per_device,
        mesh=split,
        in_specs=(rows, rows, rows, rows, P()),
        out_specs=(rows,) * 4,
        check_vma=False,
    )
```

```python
import functools

import jax
import jax.numpy as jnp
from jax import lax
from jax.experimental import pallas as pl
from jax.experimental.pallas import tpu as pltpu
from jax.sharding import Mesh, PartitionSpec as P

HD = 128
BLK = 128
SCALE = HD ** (-0.5)
LOG2E = 1.4426950408889634
NEG = -1e30

N_CC = 8
N_Y = 4
GRP = N_CC * N_Y
ROWS = 32
QB = 256
RC = 256
VM = pltpu.VMEM


def write_bias(doc, bias_ref):
    half, lead, _ = placed()
    own = [doc[half * 16 + 2 * t + lead] for t in range(N_CC)]
    other = [doc[half * 16 + 2 * t + 1 - lead] for t in range(N_CC)]
    for t in range(N_CC):
        for tk in range(t + 1):
            at = slice(tk * BLK, (tk + 1) * BLK)
            for a, keys in enumerate((own, other)):
                hidden = keys[tk] != own[t]
                if a and tk == t:
                    hidden = hidden | (lead == 0)
                value = jnp.where(hidden, NEG, 0.0)
                bias_ref[a, t : t + 1, at] = jnp.full((1, BLK), value, jnp.float32)


def pack_kernel(doc_ref, k_ref, v_ref, q_ref, g_ref, o_ref, bias_ref, buf, sems, doc, doc_sem):
    doc_copy = pltpu.make_async_copy(doc_ref, doc, doc_sem)
    doc_copy.start()
    copies = [
        pltpu.make_async_copy(ref, buf.at[a], sems.at[a])
        for a, ref in enumerate((k_ref, v_ref, q_ref, g_ref))
    ]
    for copy in copies:
        copy.start()
    doc_copy.wait()
    write_bias(doc, bias_ref)
    for a, copy in enumerate(copies):
        copy.wait()
        for h in range(GRP):
            o_ref[h, a] = buf[a, :, h * HD : (h + 1) * HD]


def unpack_kernel(x_ref, o0_ref, o1_ref, o2_ref, o3_ref, buf, sems):
    copies = [
        pltpu.make_async_copy(buf.at[a], ref, sems.at[a])
        for a, ref in enumerate((o0_ref, o1_ref, o2_ref, o3_ref))
    ]
    for a, copy in enumerate(copies):
        for h in range(GRP):
            buf[a, :, h * HD : (h + 1) * HD] = x_ref[h, a]
        copy.start()
    for copy in copies:
        copy.wait()


def dot_nt(a, b):
    return lax.dot_general(a, b, (((1,), (1,)), ((), ())), preferred_element_type=jnp.float32)


def dot_nn(a, b):
    return lax.dot_general(a, b, (((1,), (0,)), ((), ())), preferred_element_type=jnp.float32)


def placed():
    half, core = lax.axis_index("xh"), lax.axis_index("core")
    lead = jnp.where(half == core, 0, 1)
    slots = [jnp.where(half == 1, N_CC - 1 - t, t) for t in range(N_CC)]
    return half, lead, slots


def masked(s, u, bias):
    tall = []
    for i in range(2):
        wide = [
            bias(2 * u + i, tk, s[i * BLK : (i + 1) * BLK, tk * BLK : (tk + 1) * BLK])
            for tk in range(2 * u + 2)
        ]
        tall.append(jnp.concatenate(wide, axis=1))
    return jnp.concatenate(tall, axis=0)


def rows_of(u):
    return slice(u * QB, (u + 1) * QB)


def chunks(u):
    return [(low, slice(u * QB + low, u * QB + low + RC)) for low in range(0, QB, RC)]


def joined(parts):
    return [jnp.concatenate(column, axis=0) for column in zip(*parts)]


def own_kernel(bias_ref, x_ref, all_ref, e_ref, w_ref, m_ref, l_ref, o_ref):
    _, _, slots = placed()
    for t in range(N_CC):
        for a in range(4):
            all_ref[a, t * BLK : (t + 1) * BLK] = x_ref[:, slots[t], a].reshape(BLK, HD)
    below = lax.broadcasted_iota(jnp.int32, (BLK, BLK), 1) <= lax.broadcasted_iota(
        jnp.int32, (BLK, BLK), 0
    )

    def bias(t, tk, tile):
        if tk > t:
            return jnp.full_like(tile, NEG)
        if tk == t:
            return jnp.where(below, tile, NEG)
        return tile + bias_ref[0, t : t + 1, tk * BLK : (tk + 1) * BLK]

    last = N_CC // 2 - 1

    def scores(u):
        return dot_nt(all_ref[2, rows_of(u)], all_ref[0, : QB * (u + 1)])

    ready = scores(last)
    for u in reversed(range(last + 1)):
        n, r = QB * (u + 1), rows_of(u)
        s = masked(ready, u, bias)
        if u:
            ready = scores(u - 1)
        w_ref[r, :n] = dot_nt(all_ref[3, r], all_ref[1, :n])
        top = jnp.max(s, axis=1, keepdims=True)
        e = jnp.exp2((s - top) * (SCALE * LOG2E))
        e_ref[r, :n] = e
        m_ref[r] = jnp.broadcast_to(top, (QB, HD))
        l_ref[r] = jnp.broadcast_to(jnp.sum(e, axis=1, keepdims=True), (QB, HD))
        o_ref[r] = dot_nn(e.astype(jnp.bfloat16), all_ref[1, :n])


def other_kernel(
    bias_ref, all_ref, oth_ref, o_ref, m_ref, l_ref,
    out_ref, sent_ref, d_ref, k_ref, f_ref, delta_ref, v_oth, acc,
):
    _, _, slots = placed()
    for t in range(N_CC):
        k_ref[t * BLK : (t + 1) * BLK] = oth_ref[:, slots[t], 0].reshape(BLK, HD)
        v_oth[t * BLK : (t + 1) * BLK] = oth_ref[:, slots[t], 1].reshape(BLK, HD)

    def bias(t, tk, tile):
        if tk > t:
            return jnp.full_like(tile, NEG)
        return tile + bias_ref[1, t : t + 1, tk * BLK : (tk + 1) * BLK]

    last = N_CC // 2 - 1

    def scores(u):
        n, r = QB * (u + 1), rows_of(u)
        return dot_nt(all_ref[2, r], k_ref[:n])

    def weights(u):
        return dot_nt(all_ref[3, rows_of(u)], v_oth[: QB * (u + 1)])

    def softmax(u, s):
        n = QB * (u + 1)
        s = masked(s, u, bias)
        parts = []
        for low, part in chunks(u):
            piece = s[low : low + RC]
            m_own = m_ref[part, :1]
            top = jnp.maximum(m_own, jnp.max(piece, axis=1, keepdims=True))
            e = jnp.exp2((piece - top) * (SCALE * LOG2E))
            fade = jnp.exp2((m_own - top) * (SCALE * LOG2E))
            inv = 1.0 / (l_ref[part, :1] * fade + jnp.sum(e, axis=1, keepdims=True))
            fade = fade * inv
            f_ref[part] = jnp.broadcast_to(fade, (RC, HD))
            p2 = e * inv
            parts.append((p2, p2.astype(jnp.bfloat16), o_ref[part] * fade))
        return joined(parts)

    def output(u, b2, own):
        out = (own + dot_nn(b2, v_oth[: QB * (u + 1)])).astype(jnp.bfloat16)
        for i in range(2):
            out_ref[:, slots[2 * u + i]] = out[i * BLK : (i + 1) * BLK].reshape(N_Y, ROWS, HD)
        return out

    def score_grads(u, p2, w, out):
        n = QB * (u + 1)
        parts = []
        for low, part in chunks(u):
            some = slice(low, low + RC)
            g = all_ref[3, part].astype(jnp.float32)
            delta = jnp.sum(g * out[some].astype(jnp.float32), axis=1, keepdims=True)
            delta_ref[part] = jnp.broadcast_to(delta, (RC, HD))
            parts.append(((p2[some] * (w[some] - delta)).astype(jnp.bfloat16),))
        d2 = joined(parts)[0]
        d_ref[rows_of(u), :n] = d2
        return d2

    def key_grads(u, a, right):
        n, r = QB * (u + 1), rows_of(u)
        new = dot_nn(all_ref[2 + a, r].T, right)
        if u < last:
            new = acc[a, :, :n] + new
        if u:
            acc[a, :, : n - QB] = new[:, : n - QB]
        done = (new[:, n - QB :] * (1.0 if a else SCALE)).astype(jnp.bfloat16).T
        for i in range(2):
            part = done[i * BLK : (i + 1) * BLK].reshape(N_Y, ROWS, HD)
            sent_ref[:, slots[2 * u + i], a] = part

    ready = scores(last)
    kept = {}
    for u in reversed(range(last + 1)):
        s = ready
        if u:
            ready = scores(u - 1)
        p2, b2, own = softmax(u, s)
        kept[u] = p2, output(u, b2, own)
        key_grads(u, 1, b2)
    ready = weights(last)
    for u in reversed(range(last + 1)):
        w = ready
        if u:
            ready = weights(u - 1)
        p2, out = kept[u]
        key_grads(u, 0, score_grads(u, p2, w, out))


def rest_kernel(
    all_ref, k_ref, e_ref, w_ref, f_ref, delta_ref, d_ref, dq_ref, own_ref, b_own, d_own
):
    _, _, slots = placed()
    q_t, g_t = all_ref[2].T, all_ref[3].T
    for u in reversed(range(N_CC // 2)):
        n, r = QB * (u + 1), rows_of(u)
        low = u * QB
        p = e_ref[r, :n] * f_ref[r, :1]
        b_own[r, :n] = p.astype(jnp.bfloat16)
        dv = dot_nn(g_t[:, low:], b_own[low:, r])
        d = (p * (w_ref[r, :n] - delta_ref[r, :1])).astype(jnp.bfloat16)
        d_own[r, :n] = d
        dq = dot_nn(d_ref[r, :n], k_ref[:n]) + dot_nn(d, all_ref[0, :n])
        dq = (dq * SCALE).astype(jnp.bfloat16)
        dk = dot_nn(q_t[:, low:], d_own[low:, r]) * SCALE
        for i in range(2):
            at, part = slots[2 * u + i], slice(i * BLK, (i + 1) * BLK)
            dq_ref[:, at] = dq[part].reshape(N_Y, ROWS, HD)
            own_ref[:, at, 0] = dk[:, part].T.reshape(N_Y, ROWS, HD)
            own_ref[:, at, 1] = dv[:, part].T.reshape(N_Y, ROWS, HD)


def combine_kernel(out_ref, dq_ref, own_ref, recv_ref, o_ref):
    o_ref[:, :, 0] = out_ref[...]
    o_ref[:, :, 1] = dq_ref[...]
    o_ref[:, :, 2:4] = (own_ref[...] + recv_ref[...].astype(jnp.float32)).astype(jnp.bfloat16)


def whole(space=VM):
    return pl.BlockSpec(memory_space=space)


def shape(*dims, kind=jnp.bfloat16):
    return jax.ShapeDtypeStruct(dims, kind)


def near(*dims, kind=jnp.bfloat16):
    return VM(dims, kind)


def far(x):
    return pltpu.with_memory_space_constraint(x, pltpu.HBM)


def grant(mib):
    return pltpu.CompilerParams(vmem_limit_bytes=mib << 20)


def staging():
    return [VM((4, ROWS, GRP * HD), jnp.bfloat16), pltpu.SemaphoreType.DMA((4,))]


def held(x):
    return pltpu.with_memory_space_constraint(x, VM)


def per_device(queries, keys, values, grad_out, block_doc):
    full = N_CC * BLK
    packed, hide = pl.pallas_call(
        pack_kernel,
        name="pack",
        compiler_params=grant(8),
        out_shape=(near(GRP, 4, ROWS, HD), near(2, N_CC, full, kind=jnp.float32)),
        in_specs=[whole(pltpu.HBM)] * 5,
        out_specs=(whole(), whole()),
        scratch_shapes=staging()
        + [pltpu.SMEM(block_doc.shape, jnp.int32), pltpu.SemaphoreType.DMA],
    )(*[far(x) for x in (block_doc, keys, values, queries, grad_out)])
    hide = held(hide)
    mine = lax.all_to_all(packed, ("y", "cc"), 0, 0, tiled=True)
    swap = [(0, 1), (1, 0)]
    mine = mine.reshape(N_Y, N_CC, 4, ROWS, HD)
    other = lax.ppermute(mine[:, :, 0:2], "core", swap)
    f32 = jnp.float32
    everything, exps, weights, top, total, partial = pl.pallas_call(
        own_kernel,
        name="own_keys",
        compiler_params=grant(16),
        out_shape=(
            near(4, full, HD),
            near(full, full, kind=f32),
            near(full, full, kind=f32),
            near(full, HD, kind=f32),
            near(full, HD, kind=f32),
            near(full, HD, kind=f32),
        ),
        in_specs=[whole()] * 2,
        out_specs=(whole(),) * 6,
    )(hide, held(mine))
    out, sent, grads, k_other, fade, delta = pl.pallas_call(
        other_kernel,
        name="other_keys",
        compiler_params=grant(24),
        out_shape=(
            near(N_Y, N_CC, ROWS, HD),
            near(N_Y, N_CC, 2, ROWS, HD),
            near(full, full),
            near(full, HD),
            near(full, HD, kind=f32),
            near(full, HD, kind=f32),
        ),
        in_specs=[whole()] * 6,
        out_specs=(whole(),) * 6,
        scratch_shapes=[VM((full, HD), jnp.bfloat16), VM((2, HD, full), f32)],
    )(hide, *[held(x) for x in (everything, other, partial, top, total)])
    received = lax.ppermute(sent, "core", swap)
    dq, own = pl.pallas_call(
        rest_kernel,
        name="rest",
        compiler_params=grant(16),
        out_shape=(near(N_Y, N_CC, ROWS, HD), near(N_Y, N_CC, 2, ROWS, HD, kind=f32)),
        in_specs=[whole()] * 7,
        out_specs=(whole(),) * 2,
        scratch_shapes=[VM((full, full), jnp.bfloat16)] * 2,
    )(*[held(x) for x in (everything, k_other, exps, weights, fade, delta, grads)])
    back = pl.pallas_call(
        combine_kernel,
        name="combine",
        compiler_params=grant(8),
        out_shape=near(N_Y, N_CC, 4, ROWS, HD),
        in_specs=[whole()] * 4,
        out_specs=whole(),
    )(held(out), held(dq), held(own), held(received))
    back = lax.all_to_all(back.reshape(GRP, 4, ROWS, HD), ("y", "cc"), 0, 0, tiled=True)
    return tuple(
        pl.pallas_call(
            unpack_kernel,
            name="unpack",
            compiler_params=grant(8),
            out_shape=(shape(ROWS, GRP * HD),) * 4,
            in_specs=[whole()],
            out_specs=(whole(pltpu.HBM),) * 4,
            scratch_shapes=staging(),
        )(held(back))
    )


def solution(mesh):
    split = Mesh(mesh.devices.reshape(N_CC, 2, 2, N_Y), ("cc", "core", "xh", "y"))
    rows = P(("cc", "core", "xh", "y"), None)
    return jax.shard_map(
        per_device,
        mesh=split,
        in_specs=(rows, rows, rows, rows, P()),
        out_specs=(rows,) * 4,
        check_vma=False,
    )
```

```python
import functools

import jax
import jax.numpy as jnp
from jax import lax
from jax.experimental import pallas as pl
from jax.experimental.pallas import tpu as pltpu
from jax.sharding import Mesh, PartitionSpec as P

HD = 128
BLK = 128
SCALE = HD ** (-0.5)
LOG2E = 1.4426950408889634
NEG = -1e30

N_CC = 8
N_Y = 4
GRP = N_CC * N_Y
ROWS = 32
QB = 256
RC = 256
VM = pltpu.VMEM


def write_bias(doc, bias_ref):
    half, lead, _ = placed()
    own = [doc[half * 16 + 2 * t + lead] for t in range(N_CC)]
    other = [doc[half * 16 + 2 * t + 1 - lead] for t in range(N_CC)]
    for t in range(N_CC):
        for tk in range(t + 1):
            at = slice(tk * BLK, (tk + 1) * BLK)
            for a, keys in enumerate((own, other)):
                hidden = keys[tk] != own[t]
                if a and tk == t:
                    hidden = hidden | (lead == 0)
                value = jnp.where(hidden, NEG, 0.0)
                bias_ref[a, t : t + 1, at] = jnp.full((1, BLK), value, jnp.float32)


def pack_kernel(doc_ref, k_ref, v_ref, q_ref, g_ref, o_ref, bias_ref, buf, sems, doc, doc_sem):
    doc_copy = pltpu.make_async_copy(doc_ref, doc, doc_sem)
    doc_copy.start()
    copies = [
        pltpu.make_async_copy(ref, buf.at[a], sems.at[a])
        for a, ref in enumerate((k_ref, v_ref, q_ref, g_ref))
    ]
    for copy in copies:
        copy.start()
    doc_copy.wait()
    write_bias(doc, bias_ref)
    for a, copy in enumerate(copies):
        copy.wait()
        for h in range(GRP):
            o_ref[h, a] = buf[a, :, h * HD : (h + 1) * HD]


def unpack_kernel(x_ref, o0_ref, o1_ref, o2_ref, o3_ref, buf, sems):
    copies = [
        pltpu.make_async_copy(buf.at[a], ref, sems.at[a])
        for a, ref in enumerate((o0_ref, o1_ref, o2_ref, o3_ref))
    ]
    for a, copy in enumerate(copies):
        for h in range(GRP):
            buf[a, :, h * HD : (h + 1) * HD] = x_ref[h, a]
        copy.start()
    for copy in copies:
        copy.wait()


def dot_nt(a, b):
    return lax.dot_general(a, b, (((1,), (1,)), ((), ())), preferred_element_type=jnp.float32)


def dot_nn(a, b):
    return lax.dot_general(a, b, (((1,), (0,)), ((), ())), preferred_element_type=jnp.float32)


def placed():
    half, core = lax.axis_index("xh"), lax.axis_index("core")
    lead = jnp.where(half == core, 0, 1)
    slots = [jnp.where(half == 1, N_CC - 1 - t, t) for t in range(N_CC)]
    return half, lead, slots


def masked(s, u, bias):
    tall = []
    for i in range(2):
        wide = [
            bias(2 * u + i, tk, s[i * BLK : (i + 1) * BLK, tk * BLK : (tk + 1) * BLK])
            for tk in range(2 * u + 2)
        ]
        tall.append(jnp.concatenate(wide, axis=1))
    return jnp.concatenate(tall, axis=0)


def rows_of(u):
    return slice(u * QB, (u + 1) * QB)


def chunks(u):
    return [(low, slice(u * QB + low, u * QB + low + RC)) for low in range(0, QB, RC)]


def joined(parts):
    return [jnp.concatenate(column, axis=0) for column in zip(*parts)]


def own_kernel(bias_ref, x_ref, all_ref, e_ref, w_ref, m_ref, l_ref, o_ref):
    _, _, slots = placed()
    for t in range(N_CC):
        for a in range(4):
            all_ref[a, t * BLK : (t + 1) * BLK] = x_ref[:, slots[t], a].reshape(BLK, HD)
    below = lax.broadcasted_iota(jnp.int32, (BLK, BLK), 1) <= lax.broadcasted_iota(
        jnp.int32, (BLK, BLK), 0
    )

    def bias(t, tk, tile):
        if tk > t:
            return jnp.full_like(tile, NEG)
        if tk == t:
            return jnp.where(below, tile, NEG)
        return tile + bias_ref[0, t : t + 1, tk * BLK : (tk + 1) * BLK]

    last = N_CC // 2 - 1

    def scores(u):
        return dot_nt(all_ref[2, rows_of(u)], all_ref[0, : QB * (u + 1)])

    ready = scores(last)
    for u in reversed(range(last + 1)):
        n, r = QB * (u + 1), rows_of(u)
        s = masked(ready, u, bias)
        if u:
            ready = scores(u - 1)
        w_ref[r, :n] = dot_nt(all_ref[3, r], all_ref[1, :n])
        top = jnp.max(s, axis=1, keepdims=True)
        e = jnp.exp2((s - top) * (SCALE * LOG2E))
        e_ref[r, :n] = e
        m_ref[r] = jnp.broadcast_to(top, (QB, HD))
        l_ref[r] = jnp.broadcast_to(jnp.sum(e, axis=1, keepdims=True), (QB, HD))
        o_ref[r] = dot_nn(e.astype(jnp.bfloat16), all_ref[1, :n])


def other_kernel(
    bias_ref, all_ref, oth_ref, o_ref, m_ref, l_ref,
    out_ref, sent_ref, d_ref, k_ref, f_ref, delta_ref, v_oth, acc,
):
    _, _, slots = placed()
    for t in range(N_CC):
        k_ref[t * BLK : (t + 1) * BLK] = oth_ref[:, slots[t], 0].reshape(BLK, HD)
        v_oth[t * BLK : (t + 1) * BLK] = oth_ref[:, slots[t], 1].reshape(BLK, HD)

    def bias(t, tk, tile):
        if tk > t:
            return jnp.full_like(tile, NEG)
        return tile + bias_ref[1, t : t + 1, tk * BLK : (tk + 1) * BLK]

    last = N_CC // 2 - 1

    def scores(u):
        n, r = QB * (u + 1), rows_of(u)
        return dot_nt(all_ref[2, r], k_ref[:n])

    def weights(u):
        return dot_nt(all_ref[3, rows_of(u)], v_oth[: QB * (u + 1)])

    def softmax(u, s):
        n = QB * (u + 1)
        s = masked(s, u, bias)
        parts = []
        for low, part in chunks(u):
            piece = s[low : low + RC]
            m_own = m_ref[part, :1]
            top = jnp.maximum(m_own, jnp.max(piece, axis=1, keepdims=True))
            e = jnp.exp2((piece - top) * (SCALE * LOG2E))
            fade = jnp.exp2((m_own - top) * (SCALE * LOG2E))
            inv = 1.0 / (l_ref[part, :1] * fade + jnp.sum(e, axis=1, keepdims=True))
            fade = fade * inv
            f_ref[part] = jnp.broadcast_to(fade, (RC, HD))
            p2 = e * inv
            parts.append((p2, p2.astype(jnp.bfloat16), o_ref[part] * fade))
        return joined(parts)

    def output(u, b2, own):
        out = (own + dot_nn(b2, v_oth[: QB * (u + 1)])).astype(jnp.bfloat16)
        for i in range(2):
            out_ref[:, slots[2 * u + i]] = out[i * BLK : (i + 1) * BLK].reshape(N_Y, ROWS, HD)
        return out

    def score_grads(u, p2, w, out):
        n = QB * (u + 1)
        parts = []
        for low, part in chunks(u):
            some = slice(low, low + RC)
            g = all_ref[3, part].astype(jnp.float32)
            delta = jnp.sum(g * out[some].astype(jnp.float32), axis=1, keepdims=True)
            delta_ref[part] = jnp.broadcast_to(delta, (RC, HD))
            parts.append(((p2[some] * (w[some] - delta)).astype(jnp.bfloat16),))
        d2 = joined(parts)[0]
        d_ref[rows_of(u), :n] = d2
        return d2

    def key_grads(u, a, right):
        n, r = QB * (u + 1), rows_of(u)
        new = dot_nn(all_ref[2 + a, r].T, right)
        if u < last:
            new = acc[a, :, :n] + new
        if u:
            acc[a, :, : n - QB] = new[:, : n - QB]
        done = (new[:, n - QB :] * (1.0 if a else SCALE)).astype(jnp.bfloat16).T
        for i in range(2):
            part = done[i * BLK : (i + 1) * BLK].reshape(N_Y, ROWS, HD)
            sent_ref[:, slots[2 * u + i], a] = part

    ready = scores(0)
    kept = {}
    for u in range(last + 1):
        s = ready
        if u < last:
            ready = scores(u + 1)
        p2, b2, own = softmax(u, s)
        kept[u] = p2, b2, output(u, b2, own)
    ready = weights(last)
    for u in reversed(range(last + 1)):
        w = ready
        if u:
            ready = weights(u - 1)
        p2, b2, out = kept[u]
        d2 = score_grads(u, p2, w, out)
        key_grads(u, 1, b2)
        key_grads(u, 0, d2)


def rest_kernel(
    all_ref, k_ref, e_ref, w_ref, f_ref, delta_ref, d_ref, dq_ref, own_ref, b_own, d_own
):
    _, _, slots = placed()
    q_t, g_t = all_ref[2].T, all_ref[3].T
    for u in reversed(range(N_CC // 2)):
        n, r = QB * (u + 1), rows_of(u)
        low = u * QB
        p = e_ref[r, :n] * f_ref[r, :1]
        b_own[r, :n] = p.astype(jnp.bfloat16)
        dv = dot_nn(g_t[:, low:], b_own[low:, r])
        d = (p * (w_ref[r, :n] - delta_ref[r, :1])).astype(jnp.bfloat16)
        d_own[r, :n] = d
        dq = dot_nn(d_ref[r, :n], k_ref[:n]) + dot_nn(d, all_ref[0, :n])
        dq = (dq * SCALE).astype(jnp.bfloat16)
        dk = dot_nn(q_t[:, low:], d_own[low:, r]) * SCALE
        for i in range(2):
            at, part = slots[2 * u + i], slice(i * BLK, (i + 1) * BLK)
            dq_ref[:, at] = dq[part].reshape(N_Y, ROWS, HD)
            own_ref[:, at, 0] = dk[:, part].T.reshape(N_Y, ROWS, HD)
            own_ref[:, at, 1] = dv[:, part].T.reshape(N_Y, ROWS, HD)


def combine_kernel(out_ref, dq_ref, own_ref, recv_ref, o_ref):
    o_ref[:, :, 0] = out_ref[...]
    o_ref[:, :, 1] = dq_ref[...]
    o_ref[:, :, 2:4] = (own_ref[...] + recv_ref[...].astype(jnp.float32)).astype(jnp.bfloat16)


def whole(space=VM):
    return pl.BlockSpec(memory_space=space)


def shape(*dims, kind=jnp.bfloat16):
    return jax.ShapeDtypeStruct(dims, kind)


def near(*dims, kind=jnp.bfloat16):
    return VM(dims, kind)


def far(x):
    return pltpu.with_memory_space_constraint(x, pltpu.HBM)


def grant(mib):
    return pltpu.CompilerParams(vmem_limit_bytes=mib << 20)


def staging():
    return [VM((4, ROWS, GRP * HD), jnp.bfloat16), pltpu.SemaphoreType.DMA((4,))]


def held(x):
    return pltpu.with_memory_space_constraint(x, VM)


def per_device(queries, keys, values, grad_out, block_doc):
    full = N_CC * BLK
    packed, hide = pl.pallas_call(
        pack_kernel,
        name="pack",
        compiler_params=grant(8),
        out_shape=(near(GRP, 4, ROWS, HD), near(2, N_CC, full, kind=jnp.float32)),
        in_specs=[whole(pltpu.HBM)] * 5,
        out_specs=(whole(), whole()),
        scratch_shapes=staging()
        + [pltpu.SMEM(block_doc.shape, jnp.int32), pltpu.SemaphoreType.DMA],
    )(*[far(x) for x in (block_doc, keys, values, queries, grad_out)])
    hide = held(hide)
    mine = lax.all_to_all(packed, ("y", "cc"), 0, 0, tiled=True)
    swap = [(0, 1), (1, 0)]
    mine = mine.reshape(N_Y, N_CC, 4, ROWS, HD)
    other = lax.ppermute(mine[:, :, 0:2], "core", swap)
    f32 = jnp.float32
    everything, exps, weights, top, total, partial = pl.pallas_call(
        own_kernel,
        name="own_keys",
        compiler_params=grant(16),
        out_shape=(
            near(4, full, HD),
            near(full, full, kind=f32),
            near(full, full, kind=f32),
            near(full, HD, kind=f32),
            near(full, HD, kind=f32),
            near(full, HD, kind=f32),
        ),
        in_specs=[whole()] * 2,
        out_specs=(whole(),) * 6,
    )(hide, held(mine))
    out, sent, grads, k_other, fade, delta = pl.pallas_call(
        other_kernel,
        name="other_keys",
        compiler_params=grant(24),
        out_shape=(
            near(N_Y, N_CC, ROWS, HD),
            near(N_Y, N_CC, 2, ROWS, HD),
            near(full, full),
            near(full, HD),
            near(full, HD, kind=f32),
            near(full, HD, kind=f32),
        ),
        in_specs=[whole()] * 6,
        out_specs=(whole(),) * 6,
        scratch_shapes=[VM((full, HD), jnp.bfloat16), VM((2, HD, full), f32)],
    )(hide, *[held(x) for x in (everything, other, partial, top, total)])
    received = lax.ppermute(sent, "core", swap)
    dq, own = pl.pallas_call(
        rest_kernel,
        name="rest",
        compiler_params=grant(16),
        out_shape=(near(N_Y, N_CC, ROWS, HD), near(N_Y, N_CC, 2, ROWS, HD, kind=f32)),
        in_specs=[whole()] * 7,
        out_specs=(whole(),) * 2,
        scratch_shapes=[VM((full, full), jnp.bfloat16)] * 2,
    )(*[held(x) for x in (everything, k_other, exps, weights, fade, delta, grads)])
    back = pl.pallas_call(
        combine_kernel,
        name="combine",
        compiler_params=grant(8),
        out_shape=near(N_Y, N_CC, 4, ROWS, HD),
        in_specs=[whole()] * 4,
        out_specs=whole(),
    )(held(out), held(dq), held(own), held(received))
    back = lax.all_to_all(back.reshape(GRP, 4, ROWS, HD), ("y", "cc"), 0, 0, tiled=True)
    return tuple(
        pl.pallas_call(
            unpack_kernel,
            name="unpack",
            compiler_params=grant(8),
            out_shape=(shape(ROWS, GRP * HD),) * 4,
            in_specs=[whole()],
            out_specs=(whole(pltpu.HBM),) * 4,
            scratch_shapes=staging(),
        )(held(back))
    )


def solution(mesh):
    split = Mesh(mesh.devices.reshape(N_CC, 2, 2, N_Y), ("cc", "core", "xh", "y"))
    rows = P(("cc", "core", "xh", "y"), None)
    return jax.shard_map(
        per_device,
        mesh=split,
        in_specs=(rows, rows, rows, rows, P()),
        out_specs=(rows,) * 4,
        check_vma=False,
    )
```
